32 devices in a mesh: row: 8 (over z, y), col: 4 (over x, core).
Axes of the slice: x: 2, y: 2, z: 4, core: 2. Of those that a mesh axis runs over, the one named last changes fastest.
Arguments:
- ancestor_inverse: float32 [12288, 12288], P('row', 'col'), may hold values from -5 to 320, as said below
- panel_one: float32 [12288, 256], P(('row', 'col')), may hold values from -0.015625 to 0.015625
- struct_one: int32 [10752], replicated, may hold values from 0 to 12287, as said below
- lower_one: float32 [256, 256], replicated, may hold values from -1 to 2, as said below
- panel_two: float32 [12288, 256], P(('row', 'col')), may hold values from -0.015625 to 0.015625
- struct_two: int32 [9216], replicated, may hold values from 0 to 12287, as said below
- panel_above: float32 [256, 256], replicated, may hold values from -0.375 to 0.375
- lower_two: float32 [256, 256], replicated, may hold values from -1 to 2, as said below
- tile_owner: int32 [192, 1], P(('col', 'row')), may hold values from 0 to 3; in each aligned block of 6 rows (0 to 5, 6 to 11, ...) at most 2 rows name the same one
Outputs:
- inverse_one: float32 [12288, 256], P(('col', 'row'))
- diag_one: float32 [256, 256], replicated
- cross_two: float32 [256, 256], replicated
- diag_two: float32 [256, 256], replicated
- delivered: float32 [256, 64, 256], P(('row', 'col'))
The draws below stay inside these ranges and needn't reach their ends.
Inputs may be any that keep to these rules, and one draw needn't show every extreme that they name: ancestor_inverse is exactly symmetric and positive definite. `struct_one`: 10752 distinct row numbers of the ancestor block. `struct_two`: 9216 distinct entries of struct_one. `lower_one`: lower triangular with a positive diagonal. `lower_two`: lower triangular with a positive diagonal. `tile_owner`: within each aligned block of 6 entries (the tiles of one device) no value appears more than 2 times; in some block a value appears exactly 2 times.
All inputs are finite; a program needn't handle non-finite values.
Results may differ from the reference program's by a relative error of at most 0.00007.
Values sent between devices are 32-bit elements; how exact they have to be, the bound alone decides.
A program may use at most 64 MiB of HBM per device.

```python
import math
import jax
import jax.numpy as jnp
import numpy as np
from jax import lax

ANC = 12288
SUPER = 256
R_ONE = 10752
R_TWO = 9216
TILES_DEV = 6
CAP = 2
N_ROW = 8
N_COL = 4
DEVICES = 32


def draw_ancestor_inverse(key, part):
    first, second = jax.random.split(jax.random.fold_in(key, 11), 2)
    entries = jax.random.truncated_normal(first, -6.0, 6.0, (ANC, ANC), jnp.float32)
    upper_part = jnp.triu(entries, 1)
    diagonal_values = jax.random.uniform(second, (ANC,), jnp.float32, 2.5, 5.0)
    matrix = 16.0 * (jnp.diag(diagonal_values) + 0.8 / (2.0 * ANC) ** 0.5 * (upper_part + upper_part.T))
    return matrix


def structure_lists(key):
    first, second, third = jax.random.split(jax.random.fold_in(key, 23), 3)
    positions = jnp.arange(ANC, dtype=jnp.int32)
    region = positions // (ANC // 16)
    base_score = jax.random.randint(first, (ANC,), 0, 2 ** 14, dtype=jnp.int32)
    region_lift = jax.random.randint(second, (16,), 0, 2 ** 15, dtype=jnp.int32)
    scores = (base_score + region_lift[region]) * ANC + positions
    chosen = lax.top_k(scores, R_ONE)[1].astype(jnp.int32)
    shuffle = jax.random.permutation(third, R_ONE)
    return (chosen, chosen[shuffle[:R_TWO]].astype(jnp.int32))


def draw_struct_one(key, part):
    return structure_lists(key)[0]


def draw_struct_two(key, part):
    return structure_lists(key)[1]


def lower_factor(key):
    first, second = jax.random.split(key, 2)
    lower_part = jnp.tril(jax.random.truncated_normal(first, -4.0, 4.0, (SUPER, SUPER), jnp.float32) * (0.5 / SUPER ** 0.5), -1)
    diagonal_values = jnp.exp(jax.random.uniform(second, (SUPER,), jnp.float32, math.log(0.5), math.log(2.0)))
    return lower_part + jnp.diag(diagonal_values)


def draw_lower_one(key, part):
    return lower_factor(jax.random.fold_in(key, 31))


def draw_lower_two(key, part):
    return lower_factor(jax.random.fold_in(key, 37))


def level_of(own_key, dims, shards, low, high):
    def one(axis_at, shards_of):
        heights = jax.random.uniform(jax.random.fold_in(jax.random.fold_in(own_key, 6), axis_at), (shards_of,), jnp.float32, low / len(shards), high / len(shards))
        return jnp.repeat(jnp.exp(heights), dims[axis_at] // shards_of).reshape((-1,) + (1,) * (len(dims) - axis_at - 1))

    loudness = one(*shards[0])
    for cut in shards[1:]:
        loudness = loudness * one(*cut)
    return loudness


def assign_block(key, own, number, rows, amount, top, most, skew):
    ranking = jax.random.permutation(key, amount)
    heavy_load, common = shares(amount, rows * top, most, skew, True), shares(amount, rows * top, most, skew, False)
    places = jnp.arange(amount)

    def named(tallies, turn):
        used = int((tallies > 0).sum())
        fixed = max(1, used // 4)
        shifted = fixed + (places - fixed + turn * (used - fixed)) % max(1, amount - fixed)
        return jnp.zeros((amount,), jnp.int32).at[ranking[jnp.where(places < fixed, places, shifted)]].set(jnp.asarray(tallies, jnp.int32))

    tallies = jnp.where(number % 4 == 0, named(heavy_load, number // 4), named(common, number - number // 4 - 1))
    mixed = jax.random.permutation(jax.random.fold_in(own, 3), amount)
    giver, receiver = mixed[0:amount // 2 * 2:2], mixed[1:amount // 2 * 2:2]
    slack = jnp.minimum(tallies[giver] - 1, most - tallies[receiver]) // 2
    slack = jnp.where((giver == ranking[0]) | (receiver == ranking[0]) | (tallies[receiver] == 0), 0, jnp.maximum(slack, 0))
    shifted = jax.random.randint(jax.random.fold_in(own, 4), (amount // 2,), 0, 1 << 20) % (slack + 1)
    tallies = tallies.at[giver].add(-shifted).at[receiver].add(shifted)
    members = jnp.searchsorted(jnp.cumsum(tallies), jnp.arange(rows * top), side="right").astype(jnp.int32)
    grid = members.reshape(top, rows).T
    grid = grid[jax.random.permutation(jax.random.fold_in(own, 1), rows)]
    turn = jax.random.randint(jax.random.fold_in(own, 2), (rows, 1), 0, top)
    return jnp.take_along_axis(grid, (jnp.arange(top)[None, :] + turn) % top, axis=1)


def shares(count, total, bound, skew, full):
    weights = [(1 << 20) // math.isqrt(grade ** skew) + 1 for grade in range(1, count + 1)]
    largest = bound if full else min(bound, max(-(-total // count), total * weights[0] // sum(weights)))
    least = 1 if total - largest >= count - 1 else 0
    counts, rest = [largest] + [least] * (count - 1), total - largest - least * (count - 1)
    while rest > 0:
        free = [i for i in range(1, count) if counts[i] < largest] or [i for i in range(1, count) if counts[i] < bound]
        whole, left = sum([weights[i] for i in free]), rest
        for i in free:
            extra = min(bound - counts[i], max(1, left * weights[i] // whole), rest)
            counts[i] = counts[i] + extra
            rest = rest - extra
    return np.array(counts)


def normal_values(own_key, extent, deviation, limit, cuts=(), held_as=jnp.bfloat16):
    level = level_of(own_key, extent, cuts, -0.22, 0.18) if cuts else 1.0
    drawn = jax.random.normal(own_key, extent, jnp.float32) * deviation * level
    return jnp.minimum(jnp.maximum(drawn, -limit), limit).astype(held_as)


def setup_inputs(seed: int = 0) -> dict:
    splits = jax.random.split(jax.random.key(seed), 10)
    ancestor_inverse = draw_ancestor_inverse(jax.random.fold_in(splits[9], 71), 0)
    panel_one = normal_values(splits[1], (ANC, SUPER), (15 * R_ONE) ** -0.5, 0.015625, ((0, 32),), jnp.float32)
    struct_one = draw_struct_one(jax.random.fold_in(splits[9], 71), 0)
    lower_one = draw_lower_one(jax.random.fold_in(splits[9], 71), 0)
    panel_two = normal_values(splits[4], (ANC, SUPER), (15 * R_TWO) ** -0.5, 0.015625, ((0, 32),), jnp.float32)
    struct_two = draw_struct_two(jax.random.fold_in(splits[9], 71), 0)
    panel_above = normal_values(splits[6], (SUPER, SUPER), SUPER ** -0.5, 0.375, (), jnp.float32)
    lower_two = draw_lower_two(jax.random.fold_in(splits[9], 71), 0)
    tile_owner_keys = jax.random.split(jax.random.fold_in(splits[8], 1), (DEVICES * TILES_DEV) // TILES_DEV)
    tile_owner_turns = jax.random.permutation(jax.random.fold_in(splits[8], 3), (DEVICES * TILES_DEV) // TILES_DEV)
    tile_owner = jax.vmap(lambda own, number: assign_block(jax.random.fold_in(splits[8], 2), own, number, TILES_DEV, N_COL, 1, CAP, 2))(tile_owner_keys, tile_owner_turns).reshape((DEVICES * TILES_DEV, 1))
    return dict(ancestor_inverse=ancestor_inverse, panel_one=panel_one, struct_one=struct_one, lower_one=lower_one, panel_two=panel_two, struct_two=struct_two, panel_above=panel_above, lower_two=lower_two, tile_owner=tile_owner)


def matmul(left, right):
    return jnp.dot(left, right, precision=lax.Precision.HIGHEST, preferred_element_type=jnp.float32)


def deliver(values, tile_owner):
    tile_rows = ANC // (N_ROW * N_COL * TILES_DEV)
    tile_count = ANC // tile_rows
    all_tiles = values.reshape(tile_count, tile_rows, SUPER)
    owner_col = tile_owner[:, 0].astype(jnp.int32)
    onehot = (owner_col[:, None] == jnp.arange(N_COL, dtype=jnp.int32)[None, :]).astype(jnp.int32)
    grouped = onehot.reshape(tile_count // TILES_DEV, TILES_DEV, N_COL)
    earlier = jnp.cumsum(grouped, axis=1) - grouped
    tile_rank = jnp.sum(earlier * grouped, axis=2).reshape(tile_count)
    tile_group = jnp.arange(tile_count, dtype=jnp.int32) // TILES_DEV
    source_row = tile_group % N_ROW
    source_col = tile_group // N_ROW
    target = ((source_row * N_COL + owner_col) * N_COL + source_col) * CAP + tile_rank
    empty_slots = jnp.zeros((N_ROW * N_COL * N_COL * CAP, tile_rows, SUPER), jnp.float32)
    return empty_slots.at[target.astype(jnp.int32)].set(all_tiles)


def reference(ancestor_inverse, panel_one, struct_one, lower_one, panel_two, struct_two, panel_above, lower_two, tile_owner):
    mask_one = jnp.zeros((ANC,), jnp.float32).at[struct_one].set(1.0)
    mask_two = jnp.zeros((ANC,), jnp.float32).at[struct_two].set(1.0)
    masked_one = panel_one * mask_one[:, None]
    masked_two = panel_two * mask_two[:, None]
    inverse_one = -matmul(ancestor_inverse, masked_one) * mask_one[:, None]
    diag_one = matmul(lower_one.T, lower_one) - matmul(masked_one.T, inverse_one)
    inverse_two = -(matmul(ancestor_inverse, masked_two) + matmul(inverse_one, panel_above)) * mask_two[:, None]
    cross_two = -(matmul(inverse_one.T, masked_two) + matmul(diag_one, panel_above))
    diag_two = matmul(lower_two.T, lower_two) - matmul(masked_two.T, inverse_two) - matmul(panel_above.T, cross_two)
    delivered = deliver(inverse_two, tile_owner)
    return inverse_one, diag_one, cross_two, diag_two, delivered
```

```python
import jax
import jax.numpy as jnp
from jax import lax
from jax.sharding import PartitionSpec as P

CAP = 2


def matmul(left, right):
    return jnp.dot(left, right, precision=lax.Precision.HIGHEST, preferred_element_type=jnp.float32)


def contract_rows(left, right, precision=lax.Precision.HIGHEST):
    return lax.dot_general(
        left,
        right,
        (((0,), (0,)), ((), ())),
        precision=precision,
        preferred_element_type=jnp.float32,
    )


def row_mask(struct, count):
    lanes = 128
    high = struct // lanes
    low = struct % lanes
    high_hot = (jnp.arange(count // lanes, dtype=jnp.int32)[:, None] == high[None, :]).astype(jnp.bfloat16)
    low_hot = (jnp.arange(lanes, dtype=jnp.int32)[:, None] == low[None, :]).astype(jnp.bfloat16)
    counts = lax.dot_general(high_hot, low_hot, (((1,), (1,)), ((), ())), preferred_element_type=jnp.float32)
    return (counts > 0.5).astype(jnp.float32).reshape(count)


def deliver(values, tile_owner, col_count):
    tile_count = tile_owner.shape[0]
    tile_rows = values.shape[0] // tile_count
    all_tiles = values.reshape(tile_count, tile_rows, values.shape[1])
    owner_col = tile_owner[:, 0]
    col_ids = jnp.arange(col_count, dtype=jnp.int32)
    onehot = (owner_col[:, None] == col_ids[None, :]).astype(jnp.int32)
    tile_rank = jnp.sum((jnp.cumsum(onehot, axis=0) - onehot) * onehot, axis=1)
    slot_index = jnp.arange(CAP, dtype=jnp.int32)
    select = (
        (owner_col[None, None, :] == col_ids[:, None, None])
        & (tile_rank[None, None, :] == slot_index[None, :, None])
    ).astype(jnp.float32)
    outgoing = jnp.einsum("cks,srb->ckrb", select, all_tiles, precision=lax.Precision.HIGHEST)
    incoming = lax.all_to_all(outgoing, "col", split_axis=0, concat_axis=0, tiled=True)
    return incoming.reshape(col_count * CAP, tile_rows, values.shape[1])


def local(
    ancestor_inverse,
    panel_one,
    struct_one,
    lower_one,
    panel_two,
    struct_two,
    panel_above,
    lower_two,
    tile_owner,
):
    row_count = lax.axis_size("row")
    col_count = lax.axis_size("col")
    row_index = lax.axis_index("row")
    col_index = lax.axis_index("col")
    local_rows = panel_one.shape[0]
    order = local_rows * row_count * col_count
    width = panel_one.shape[1]
    mask_one = row_mask(struct_one, order)
    mask_two = row_mask(struct_two, order)
    panel_start = (row_index * col_count + col_index) * local_rows
    result_start = (col_index * row_count + row_index) * local_rows
    local_one = panel_one * lax.dynamic_slice_in_dim(mask_one, panel_start, local_rows)[:, None]
    local_two = panel_two * lax.dynamic_slice_in_dim(mask_two, panel_start, local_rows)[:, None]
    result_mask_one = lax.dynamic_slice_in_dim(mask_one, result_start, local_rows)[:, None]
    result_mask_two = lax.dynamic_slice_in_dim(mask_two, result_start, local_rows)[:, None]

    both = jnp.concatenate([local_one, local_two], axis=1)
    gathered = lax.all_gather(both, "col", axis=0, tiled=True)
    moves = [(f, (f % row_count) * col_count + f // row_count) for f in range(row_count * col_count)]
    resident = lax.ppermute(both, ("row", "col"), moves)
    product = lax.psum_scatter(
        contract_rows(ancestor_inverse, gathered, lax.Precision.HIGH),
        "row",
        scatter_dimension=0,
        tiled=True,
    )
    resident_one = resident[:, :width]
    resident_two = resident[:, width:]
    inverse_one = -product[:, :width] * result_mask_one
    inverse_two = -(product[:, width:] + matmul(inverse_one, panel_above)) * result_mask_two
    sums = lax.psum(
        jnp.concatenate(
            [
                contract_rows(resident_one, inverse_one),
                contract_rows(inverse_one, resident_two),
                contract_rows(resident_two, inverse_two),
            ],
            axis=1,
        ),
        ("row", "col"),
    )
    gram_one = sums[:, :width]
    cross_sum = sums[:, width : 2 * width]
    gram_two = sums[:, 2 * width :]
    diag_one = matmul(lower_one.T, lower_one) - gram_one
    cross_two = -(cross_sum + matmul(diag_one, panel_above))
    diag_two = matmul(lower_two.T, lower_two) - gram_two - matmul(panel_above.T, cross_two)
    delivered = deliver(inverse_two, tile_owner, col_count)
    return (inverse_one, diag_one, cross_two, diag_two, delivered)


def solution(mesh):
    return jax.shard_map(
        local,
        mesh=mesh,
        in_specs=(
            P("row", "col"),
            P(("row", "col"), None),
            P(),
            P(),
            P(("row", "col"), None),
            P(),
            P(),
            P(),
            P(("col", "row"), None),
        ),
        out_specs=(P(("col", "row"), None), P(), P(), P(), P(("row", "col"), None, None)),
        check_vma=False,
    )
```

```python
import functools

import jax
import jax.numpy as jnp
from jax import lax
from jax.experimental import pallas as pl
from jax.experimental.pallas import tpu as pltpu
from jax.sharding import PartitionSpec as P

CAP = 2


def matmul(left, right):
    return jnp.dot(left, right, precision=lax.Precision.HIGHEST, preferred_element_type=jnp.float32)


def contract_rows(left, right, precision=lax.Precision.HIGHEST):
    return lax.dot_general(
        left,
        right,
        (((0,), (0,)), ((), ())),
        precision=precision,
        preferred_element_type=jnp.float32,
    )


def row_mask(struct, count):
    lanes = 128
    high = struct // lanes
    low = struct % lanes
    high_hot = (jnp.arange(count // lanes, dtype=jnp.int32)[:, None] == high[None, :]).astype(jnp.bfloat16)
    low_hot = (jnp.arange(lanes, dtype=jnp.int32)[:, None] == low[None, :]).astype(jnp.bfloat16)
    counts = lax.dot_general(high_hot, low_hot, (((1,), (1,)), ((), ())), preferred_element_type=jnp.float32)
    return (counts > 0.5).astype(jnp.float32).reshape(count)


MESH = pl.DeviceIdType.MESH


def greet(peers):
    barrier = pltpu.get_barrier_semaphore()
    for peer in peers:
        pl.semaphore_signal(barrier, inc=1, device_id=peer, device_id_type=MESH)
    pl.semaphore_wait(barrier, len(peers))


def scatter_kernel(rows, value_ref, out_ref, pair_in, total, major_in, pair_send, pair_recv, major_send, major_recv):
    majors = rows // 2
    row = lax.axis_index("row")
    col = lax.axis_index("col")
    major, minor = row // 2, row % 2
    partner = (major * 2 + 1 - minor, col)

    def peer(offset):
        return (lax.rem(major + offset, majors) * 2 + minor, col)

    greet([partner] + [peer(offset) for offset in range(1, majors)])
    order = sorted(range(1, majors), key=lambda offset: -min(offset, majors - offset)) + [0]
    started = []
    pair_copies = {}
    for offset in order:
        target = lax.rem(major + offset, majors)
        copy = pltpu.make_async_remote_copy(
            src_ref=value_ref.at[target * 2 + 1 - minor],
            dst_ref=pair_in.at[offset],
            send_sem=pair_send.at[offset],
            recv_sem=pair_recv.at[offset],
            device_id=partner,
            device_id_type=MESH,
        )
        copy.start()
        pair_copies[offset] = copy
    for offset in order:
        target = lax.rem(major + offset, majors)
        pair_copies[offset].wait_recv()
        total[offset] = pair_in[offset] + value_ref[target * 2 + minor]
        if offset:
            copy = pltpu.make_async_remote_copy(
                src_ref=total.at[offset],
                dst_ref=major_in.at[offset - 1],
                send_sem=major_send.at[offset - 1],
                recv_sem=major_recv.at[offset - 1],
                device_id=peer(offset),
                device_id_type=MESH,
            )
            copy.start()
            started.append(copy)
    for copy in started:
        copy.wait_recv()
    result = total[0]
    for slot in range(majors - 1):
        result = result + major_in[slot]
    out_ref[...] = result
    for copy in started:
        copy.wait_send()
    for offset in order:
        pair_copies[offset].wait_send()


def scatter_rows(value, rows):
    chunk, width = value.shape[0] // rows, value.shape[1]
    majors = rows // 2
    dma = pltpu.SemaphoreType.DMA
    return pl.pallas_call(
        functools.partial(scatter_kernel, rows),
        out_shape=jax.ShapeDtypeStruct((chunk, width), jnp.float32),
        in_specs=[pl.BlockSpec(memory_space=pltpu.VMEM)],
        out_specs=pl.BlockSpec(memory_space=pltpu.VMEM),
        scratch_shapes=[
            pltpu.VMEM((majors, chunk, width), jnp.float32),
            pltpu.VMEM((majors, chunk, width), jnp.float32),
            pltpu.VMEM((majors - 1, chunk, width), jnp.float32),
            dma((majors,)),
            dma((majors,)),
            dma((majors - 1,)),
            dma((majors - 1,)),
        ],
        compiler_params=pltpu.CompilerParams(
            collective_id=0, has_side_effects=True, vmem_limit_bytes=40 * 2**20
        ),
    )(value.reshape(rows, chunk, width))


def sum_kernel(rows, cols, value_ref, out_ref, full, sum_a, sum_b, in_a, in_b, in_c, *sems):
    row = lax.axis_index("row")
    col = lax.axis_index("col")
    outer = cols // 2
    far, core = col // 2, col % 2
    half = outer * rows
    base_a = core * half
    base_b = base_a + far * rows
    base_c = base_b + row

    def pair_peer(offset):
        return (row, far * 2 + 1 - core)

    def far_peer(offset):
        return (row, lax.rem(far + offset, outer) * 2 + core)

    def row_peer(offset):
        return (lax.rem(row + offset, rows), col)

    greet(
        [pair_peer(1)]
        + [far_peer(offset) for offset in range(1, outer)]
        + [row_peer(offset) for offset in range(1, rows)]
    )

    def exchange(count, peer, source, landing, stage):
        copies = []
        for offset in range(1, count):
            copy = pltpu.make_async_remote_copy(
                src_ref=source(offset),
                dst_ref=landing(offset),
                send_sem=sems[2 * stage].at[offset - 1],
                recv_sem=sems[2 * stage + 1].at[offset - 1],
                device_id=peer(offset),
                device_id_type=MESH,
            )
            copy.start()
            copies.append(copy)
        for copy in copies:
            copy.wait_recv()
        return copies

    pending = []
    pending += exchange(
        2, pair_peer, lambda k: value_ref.at[pl.ds((1 - core) * half, half)], lambda k: in_a.at[k - 1], 0
    )
    sum_a[...] = value_ref[pl.ds(base_a, half)] + in_a[0]
    pending += exchange(
        outer, far_peer, lambda k: sum_a.at[pl.ds(lax.rem(far + k, outer) * rows, rows)], lambda k: in_b.at[k - 1], 1
    )
    total = sum_a[pl.ds(far * rows, rows)]
    for slot in range(outer - 1):
        total = total + in_b[slot]
    sum_b[...] = total
    pending += exchange(
        rows, row_peer, lambda k: sum_b.at[lax.rem(row + k, rows)], lambda k: in_c.at[k - 1], 2
    )
    total = sum_b[row]
    for slot in range(rows - 1):
        total = total + in_c[slot]
    full[base_c] = total
    pending += exchange(rows, row_peer, lambda k: full.at[base_c], lambda k: full.at[base_c], 3)
    pending += exchange(
        outer, far_peer, lambda k: full.at[pl.ds(base_b, rows)], lambda k: full.at[pl.ds(base_b, rows)], 4
    )
    pending += exchange(
        2, pair_peer, lambda k: full.at[pl.ds(base_a, half)], lambda k: full.at[pl.ds(base_a, half)], 5
    )
    out_ref[...] = full[...]
    for copy in pending:
        copy.wait_send()


def sum_everywhere(value, rows, cols):
    devices = rows * cols
    lanes = value.shape[1]
    depth = value.shape[0] // devices
    outer = cols // 2
    dma = pltpu.SemaphoreType.DMA
    vmem = lambda *lead: pltpu.VMEM(lead + (depth, lanes), jnp.float32)
    total = pl.pallas_call(
        functools.partial(sum_kernel, rows, cols),
        out_shape=jax.ShapeDtypeStruct((devices, depth, lanes), jnp.float32),
        in_specs=[pl.BlockSpec(memory_space=pltpu.VMEM)],
        out_specs=pl.BlockSpec(memory_space=pltpu.VMEM),
        scratch_shapes=[
            vmem(devices),
            vmem(devices // 2),
            vmem(rows),
            vmem(1, devices // 2),
            vmem(outer - 1, rows),
            vmem(rows - 1),
        ]
        + [dma((count - 1,)) for count in (2, outer, rows, rows, outer, 2) for _ in range(2)],
        compiler_params=pltpu.CompilerParams(
            collective_id=1, has_side_effects=True, vmem_limit_bytes=24 * 2**20
        ),
    )(value.reshape(devices, depth, lanes))
    return total.reshape(value.shape)


def deliver(values, tile_owner, col_count):
    tile_count = tile_owner.shape[0]
    tile_rows = values.shape[0] // tile_count
    all_tiles = values.reshape(tile_count, tile_rows, values.shape[1])
    owner_col = tile_owner[:, 0]
    col_ids = jnp.arange(col_count, dtype=jnp.int32)
    onehot = (owner_col[:, None] == col_ids[None, :]).astype(jnp.int32)
    tile_rank = jnp.sum((jnp.cumsum(onehot, axis=0) - onehot) * onehot, axis=1)
    slot_index = jnp.arange(CAP, dtype=jnp.int32)
    select = (
        (owner_col[None, None, :] == col_ids[:, None, None])
        & (tile_rank[None, None, :] == slot_index[None, :, None])
    ).astype(jnp.float32)
    outgoing = jnp.einsum("cks,srb->ckrb", select, all_tiles, precision=lax.Precision.HIGHEST)
    incoming = lax.all_to_all(outgoing, "col", split_axis=0, concat_axis=0, tiled=True)
    return incoming.reshape(col_count * CAP, tile_rows, values.shape[1])


def local(
    ancestor_inverse,
    panel_one,
    struct_one,
    lower_one,
    panel_two,
    struct_two,
    panel_above,
    lower_two,
    tile_owner,
):
    row_count = lax.axis_size("row")
    col_count = lax.axis_size("col")
    row_index = lax.axis_index("row")
    col_index = lax.axis_index("col")
    local_rows = panel_one.shape[0]
    order = local_rows * row_count * col_count
    width = panel_one.shape[1]
    mask_one = row_mask(struct_one, order)
    mask_two = row_mask(struct_two, order)
    panel_start = (row_index * col_count + col_index) * local_rows
    result_start = (col_index * row_count + row_index) * local_rows
    local_one = panel_one * lax.dynamic_slice_in_dim(mask_one, panel_start, local_rows)[:, None]
    local_two = panel_two * lax.dynamic_slice_in_dim(mask_two, panel_start, local_rows)[:, None]
    result_mask_one = lax.dynamic_slice_in_dim(mask_one, result_start, local_rows)[:, None]
    result_mask_two = lax.dynamic_slice_in_dim(mask_two, result_start, local_rows)[:, None]

    both = jnp.concatenate([local_one, local_two], axis=1)
    gathered = lax.all_gather(both, "col", axis=0, tiled=True)
    moves = [(f, (f % row_count) * col_count + f // row_count) for f in range(row_count * col_count)]
    resident = lax.ppermute(both, ("row", "col"), moves)
    product = scatter_rows(contract_rows(ancestor_inverse, gathered, lax.Precision.HIGH), row_count)
    resident_one = resident[:, :width]
    resident_two = resident[:, width:]
    inverse_one = -product[:, :width] * result_mask_one
    inverse_two = -(product[:, width:] + matmul(inverse_one, panel_above)) * result_mask_two
    grams = (
        contract_rows(resident_one, inverse_one),
        contract_rows(inverse_one, resident_two),
        contract_rows(resident_two, inverse_two),
    )
    lanes = 128
    packed = jnp.concatenate(
        [gram[:, at : at + lanes] for gram in grams for at in range(0, width, lanes)], axis=0
    )
    sums = sum_everywhere(packed, row_count, col_count).reshape(len(grams), width // lanes, width, lanes)
    gram_one, cross_sum, gram_two = (
        jnp.concatenate([sums[at, block] for block in range(width // lanes)], axis=1) for at in range(len(grams))
    )
    diag_one = matmul(lower_one.T, lower_one) - gram_one
    cross_two = -(cross_sum + matmul(diag_one, panel_above))
    diag_two = matmul(lower_two.T, lower_two) - gram_two - matmul(panel_above.T, cross_two)
    delivered = deliver(inverse_two, tile_owner, col_count)
    return (inverse_one, diag_one, cross_two, diag_two, delivered)


def solution(mesh):
    return jax.shard_map(
        local,
        mesh=mesh,
        in_specs=(
            P("row", "col"),
            P(("row", "col"), None),
            P(),
            P(),
            P(("row", "col"), None),
            P(),
            P(),
            P(),
            P(("col", "row"), None),
        ),
        out_specs=(P(("col", "row"), None), P(), P(), P(), P(("row", "col"), None, None)),
        check_vma=False,
    )
```

```python
import functools

import jax
import jax.numpy as jnp
from jax import lax
from jax.experimental import pallas as pl
from jax.experimental.pallas import tpu as pltpu
from jax.sharding import PartitionSpec as P

CAP = 2


def matmul(left, right):
    return jnp.dot(left, right, precision=lax.Precision.HIGHEST, preferred_element_type=jnp.float32)


def contract_rows(left, right, precision=lax.Precision.HIGHEST):
    return lax.dot_general(
        left,
        right,
        (((0,), (0,)), ((), ())),
        precision=precision,
        preferred_element_type=jnp.float32,
    )


def row_mask(struct, count):
    lanes = 128
    high = struct // lanes
    low = struct % lanes
    high_hot = (jnp.arange(count // lanes, dtype=jnp.int32)[:, None] == high[None, :]).astype(jnp.bfloat16)
    low_hot = (jnp.arange(lanes, dtype=jnp.int32)[:, None] == low[None, :]).astype(jnp.bfloat16)
    counts = lax.dot_general(high_hot, low_hot, (((1,), (1,)), ((), ())), preferred_element_type=jnp.float32)
    return (counts > 0.5).astype(jnp.float32).reshape(count)


MESH = pl.DeviceIdType.MESH


def greet(peers):
    barrier = pltpu.get_barrier_semaphore()
    for peer in peers:
        pl.semaphore_signal(barrier, inc=1, device_id=peer, device_id_type=MESH)
    pl.semaphore_wait(barrier, len(peers))


def scatter_kernel(rows, value_ref, out_ref, pair_in, total, major_in, pair_send, pair_recv, major_send, major_recv):
    majors = rows // 2
    row = lax.axis_index("row")
    col = lax.axis_index("col")
    major, minor = row // 2, row % 2
    partner = (major * 2 + 1 - minor, col)

    def peer(offset):
        return (lax.rem(major + offset, majors) * 2 + minor, col)

    greet([partner] + [peer(offset) for offset in range(1, majors)])
    order = sorted(range(1, majors), key=lambda offset: -min(offset, majors - offset)) + [0]
    started = []
    pair_copies = {}
    for offset in order:
        target = lax.rem(major + offset, majors)
        copy = pltpu.make_async_remote_copy(
            src_ref=value_ref.at[target * 2 + 1 - minor],
            dst_ref=pair_in.at[offset],
            send_sem=pair_send.at[offset],
            recv_sem=pair_recv.at[offset],
            device_id=partner,
            device_id_type=MESH,
        )
        copy.start()
        pair_copies[offset] = copy
    for offset in order:
        target = lax.rem(major + offset, majors)
        pair_copies[offset].wait_recv()
        total[offset] = pair_in[offset] + value_ref[target * 2 + minor]
        if offset:
            copy = pltpu.make_async_remote_copy(
                src_ref=total.at[offset],
                dst_ref=major_in.at[offset - 1],
                send_sem=major_send.at[offset - 1],
                recv_sem=major_recv.at[offset - 1],
                device_id=peer(offset),
                device_id_type=MESH,
            )
            copy.start()
            started.append(copy)
    for copy in started:
        copy.wait_recv()
    result = total[0]
    for slot in range(majors - 1):
        result = result + major_in[slot]
    out_ref[...] = result
    for copy in started:
        copy.wait_send()
    for offset in order:
        pair_copies[offset].wait_send()


def scatter_rows(value, rows):
    chunk, width = value.shape[0] // rows, value.shape[1]
    majors = rows // 2
    dma = pltpu.SemaphoreType.DMA
    return pl.pallas_call(
        functools.partial(scatter_kernel, rows),
        out_shape=jax.ShapeDtypeStruct((chunk, width), jnp.float32),
        in_specs=[pl.BlockSpec(memory_space=pltpu.VMEM)],
        out_specs=pl.BlockSpec(memory_space=pltpu.VMEM),
        scratch_shapes=[
            pltpu.VMEM((majors, chunk, width), jnp.float32),
            pltpu.VMEM((majors, chunk, width), jnp.float32),
            pltpu.VMEM((majors - 1, chunk, width), jnp.float32),
            dma((majors,)),
            dma((majors,)),
            dma((majors - 1,)),
            dma((majors - 1,)),
        ],
        compiler_params=pltpu.CompilerParams(
            collective_id=0, has_side_effects=True, vmem_limit_bytes=40 * 2**20
        ),
    )(value.reshape(rows, chunk, width))


def gather_kernel(cols, parts, block_ref, high_ref, low_ref, held, pair_send, pair_recv, far_send, far_recv, relay_send, relay_recv):
    row = lax.axis_index("row")
    col = lax.axis_index("col")
    outer = cols // 2
    far, core = col // 2, col % 2
    partner = (row, far * 2 + 1 - core)

    def far_peer(offset):
        return (row, lax.rem(far + offset, outer) * 2 + core)

    greet([partner] + [far_peer(offset) for offset in range(1, outer)])

    def send(source, slot, part, target, send_sem, recv_sem):
        copy = pltpu.make_async_remote_copy(
            src_ref=source,
            dst_ref=held.at[slot, part],
            send_sem=send_sem,
            recv_sem=recv_sem,
            device_id=target,
            device_id_type=MESH,
        )
        copy.start()
        return copy

    far_copies = [
        (offset, part, send(
            block_ref.at[part], col, part, far_peer(offset), far_send.at[offset - 1, part], far_recv.at[offset - 1, part]
        ))
        for part in range(parts)
        for offset in range(1, outer)
    ]
    pair_copies = [
        send(block_ref.at[part], col, part, partner, pair_send.at[part], pair_recv.at[part]) for part in range(parts)
    ]
    relays = []
    for offset, part, copy in far_copies:
        copy.wait_recv()
        source = lax.rem(far - offset + outer, outer) * 2 + core
        relays.append(
            send(
                held.at[source, part],
                source,
                part,
                partner,
                relay_send.at[offset - 1, part],
                relay_recv.at[offset - 1, part],
            )
        )
    held[col] = block_ref[...]
    for copy in pair_copies + relays:
        copy.wait_recv()
    height, length = block_ref.shape[1:]
    for slot in range(cols):
        for part in range(parts):
            value = held[slot, part]
            high = value.astype(jnp.bfloat16)
            place = (pl.ds(part * height, height), pl.ds(slot * length, length))
            high_ref[place] = high
            low_ref[place] = (value - high.astype(jnp.float32)).astype(jnp.bfloat16)
    for copy in pair_copies + relays + [entry[2] for entry in far_copies]:
        copy.wait_send()


def gather_columns(block, cols):
    parts = 2
    width, length = block.shape
    outer = cols // 2
    dma = pltpu.SemaphoreType.DMA
    return pl.pallas_call(
        functools.partial(gather_kernel, cols, parts),
        out_shape=[jax.ShapeDtypeStruct((width, cols * length), jnp.bfloat16)] * 2,
        in_specs=[pl.BlockSpec(memory_space=pltpu.VMEM)],
        out_specs=[pl.BlockSpec(memory_space=pltpu.VMEM)] * 2,
        scratch_shapes=[pltpu.VMEM((cols, parts, width // parts, length), jnp.float32)]
        + [dma((parts,))] * 2
        + [dma((outer - 1, parts))] * 4,
        compiler_params=pltpu.CompilerParams(
            collective_id=2, has_side_effects=True, vmem_limit_bytes=24 * 2**20
        ),
    )(block.reshape(parts, width // parts, length))


def product_kernel(
    rows, matrix_ref, high_ref, low_ref, out_ref, window, mine, other, pair_in, major_in,
    window_sem, pair_send, pair_recv, major_send, major_recv,
):
    majors = rows // 2
    row = lax.axis_index("row")
    col = lax.axis_index("col")
    major, minor = row // 2, row % 2
    partner = (major * 2 + 1 - minor, col)
    span = out_ref.shape[1]

    def peer(offset):
        return (lax.rem(major + offset, majors) * 2 + minor, col)

    def fetch(step, which):
        target = lax.rem(major + step + 1, majors) * 2 + lax.rem(1 - minor + which, 2)
        return pltpu.make_async_copy(
            matrix_ref.at[:, pl.ds(pl.multiple_of(target * span, 128), span)],
            window.at[which],
            window_sem.at[which],
        )

    def pair_copy(step):
        return pltpu.make_async_remote_copy(
            src_ref=other.at[step],
            dst_ref=pair_in.at[step],
            send_sem=pair_send.at[step],
            recv_sem=pair_recv.at[step],
            device_id=partner,
            device_id_type=MESH,
        )

    for which in range(2):
        fetch(0, which).start()
    greet([partner] + [peer(offset) for offset in range(1, majors)])

    def dot(left, right):
        return jnp.dot(left, right, preferred_element_type=jnp.float32)

    def body(step, carry):
        for which, result in enumerate((other, mine)):
            fetch(step, which).wait()
            value = window[which]
            high = value.astype(jnp.bfloat16)
            low = (value - high.astype(jnp.float32)).astype(jnp.bfloat16)
            result[step] = dot(high_ref[...], high) + (dot(high_ref[...], low) + dot(low_ref[...], high))

            @pl.when(step + 1 < majors)
            def _():
                fetch(step + 1, which).start()

            if which == 0:
                pair_copy(step).start()
        return carry

    lax.fori_loop(0, majors, body, 0)
    started = []
    for step in range(majors):
        pair_copy(step).wait_recv()
        mine[step] = mine[step] + pair_in[step]
        if step + 1 < majors:
            copy = pltpu.make_async_remote_copy(
                src_ref=mine.at[step],
                dst_ref=major_in.at[step],
                send_sem=major_send.at[step],
                recv_sem=major_recv.at[step],
                device_id=peer(step + 1),
                device_id_type=MESH,
            )
            copy.start()
            started.append(copy)
    for copy in started:
        copy.wait_recv()
    result = mine[majors - 1]
    for slot in range(majors - 1):
        result = result + major_in[slot]
    out_ref[...] = result
    for copy in started:
        copy.wait_send()
    for step in range(majors):
        pair_copy(step).wait_send()


def product_rows(matrix, high, low, rows):
    width = high.shape[0]
    depth = matrix.shape[0]
    span = matrix.shape[1] // rows
    majors = rows // 2
    dma = pltpu.SemaphoreType.DMA
    vmem = lambda *shape: pltpu.VMEM(shape, jnp.float32)
    return pl.pallas_call(
        functools.partial(product_kernel, rows),
        out_shape=jax.ShapeDtypeStruct((width, span), jnp.float32),
        in_specs=[pl.BlockSpec(memory_space=pl.ANY)] + [pl.BlockSpec(memory_space=pltpu.VMEM)] * 2,
        out_specs=pl.BlockSpec(memory_space=pltpu.VMEM),
        scratch_shapes=[
            vmem(2, depth, span),
            vmem(majors, width, span),
            vmem(majors, width, span),
            vmem(majors, width, span),
            vmem(majors - 1, width, span),
            dma((2,)),
            dma((majors,)),
            dma((majors,)),
            dma((majors - 1,)),
            dma((majors - 1,)),
        ],
        compiler_params=pltpu.CompilerParams(
            collective_id=0, has_side_effects=True, vmem_limit_bytes=48 * 2**20
        ),
    )(matrix, high, low)


def sum_kernel(rows, cols, value_ref, out_ref, full, sum_a, sum_b, in_a, in_b, in_c, *sems):
    row = lax.axis_index("row")
    col = lax.axis_index("col")
    outer = cols // 2
    far, core = col // 2, col % 2
    half = outer * rows
    base_a = core * half
    base_b = base_a + far * rows
    base_c = base_b + row

    def pair_peer(offset):
        return (row, far * 2 + 1 - core)

    def far_peer(offset):
        return (row, lax.rem(far + offset, outer) * 2 + core)

    def row_peer(offset):
        return (lax.rem(row + offset, rows), col)

    greet(
        [pair_peer(1)]
        + [far_peer(offset) for offset in range(1, outer)]
        + [row_peer(offset) for offset in range(1, rows)]
    )

    def exchange(count, peer, source, landing, stage):
        copies = []
        for offset in range(1, count):
            copy = pltpu.make_async_remote_copy(
                src_ref=source(offset),
                dst_ref=landing(offset),
                send_sem=sems[2 * stage].at[offset - 1],
                recv_sem=sems[2 * stage + 1].at[offset - 1],
                device_id=peer(offset),
                device_id_type=MESH,
            )
            copy.start()
            copies.append(copy)
        for copy in copies:
            copy.wait_recv()
        return copies

    pending = []
    pending += exchange(
        2, pair_peer, lambda k: value_ref.at[pl.ds((1 - core) * half, half)], lambda k: in_a.at[k - 1], 0
    )
    sum_a[...] = value_ref[pl.ds(base_a, half)] + in_a[0]
    pending += exchange(
        outer, far_peer, lambda k: sum_a.at[pl.ds(lax.rem(far + k, outer) * rows, rows)], lambda k: in_b.at[k - 1], 1
    )
    total = sum_a[pl.ds(far * rows, rows)]
    for slot in range(outer - 1):
        total = total + in_b[slot]
    sum_b[...] = total
    pending += exchange(
        rows, row_peer, lambda k: sum_b.at[lax.rem(row + k, rows)], lambda k: in_c.at[k - 1], 2
    )
    total = sum_b[row]
    for slot in range(rows - 1):
        total = total + in_c[slot]
    full[base_c] = total
    pending += exchange(rows, row_peer, lambda k: full.at[base_c], lambda k: full.at[base_c], 3)
    pending += exchange(
        outer, far_peer, lambda k: full.at[pl.ds(base_b, rows)], lambda k: full.at[pl.ds(base_b, rows)], 4
    )
    pending += exchange(
        2, pair_peer, lambda k: full.at[pl.ds(base_a, half)], lambda k: full.at[pl.ds(base_a, half)], 5
    )
    out_ref[...] = full[...]
    for copy in pending:
        copy.wait_send()


def sum_everywhere(value, rows, cols):
    devices = rows * cols
    lanes = value.shape[1]
    depth = value.shape[0] // devices
    outer = cols // 2
    dma = pltpu.SemaphoreType.DMA
    vmem = lambda *lead: pltpu.VMEM(lead + (depth, lanes), jnp.float32)
    total = pl.pallas_call(
        functools.partial(sum_kernel, rows, cols),
        out_shape=jax.ShapeDtypeStruct((devices, depth, lanes), jnp.float32),
        in_specs=[pl.BlockSpec(memory_space=pltpu.VMEM)],
        out_specs=pl.BlockSpec(memory_space=pltpu.VMEM),
        scratch_shapes=[
            vmem(devices),
            vmem(devices // 2),
            vmem(rows),
            vmem(1, devices // 2),
            vmem(outer - 1, rows),
            vmem(rows - 1),
        ]
        + [dma((count - 1,)) for count in (2, outer, rows, rows, outer, 2) for _ in range(2)],
        compiler_params=pltpu.CompilerParams(
            collective_id=1, has_side_effects=True, vmem_limit_bytes=24 * 2**20
        ),
    )(value.reshape(devices, depth, lanes))
    return total.reshape(value.shape)


def deliver(values, tile_owner, col_count):
    tile_count = tile_owner.shape[0]
    tile_rows = values.shape[0] // tile_count
    all_tiles = values.reshape(tile_count, tile_rows, values.shape[1])
    owner_col = tile_owner[:, 0]
    col_ids = jnp.arange(col_count, dtype=jnp.int32)
    onehot = (owner_col[:, None] == col_ids[None, :]).astype(jnp.int32)
    tile_rank = jnp.sum((jnp.cumsum(onehot, axis=0) - onehot) * onehot, axis=1)
    slot_index = jnp.arange(CAP, dtype=jnp.int32)
    select = (
        (owner_col[None, None, :] == col_ids[:, None, None])
        & (tile_rank[None, None, :] == slot_index[None, :, None])
    ).astype(jnp.float32)
    outgoing = jnp.einsum("cks,srb->ckrb", select, all_tiles, precision=lax.Precision.HIGHEST)
    incoming = lax.all_to_all(outgoing, "col", split_axis=0, concat_axis=0, tiled=True)
    return incoming.reshape(col_count * CAP, tile_rows, values.shape[1])


def local(
    ancestor_inverse,
    panel_one,
    struct_one,
    lower_one,
    panel_two,
    struct_two,
    panel_above,
    lower_two,
    tile_owner,
):
    row_count = lax.axis_size("row")
    col_count = lax.axis_size("col")
    row_index = lax.axis_index("row")
    col_index = lax.axis_index("col")
    local_rows = panel_one.shape[0]
    order = local_rows * row_count * col_count
    width = panel_one.shape[1]
    mask_one = row_mask(struct_one, order)
    mask_two = row_mask(struct_two, order)
    panel_start = (row_index * col_count + col_index) * local_rows
    result_start = (col_index * row_count + row_index) * local_rows
    local_one = panel_one * lax.dynamic_slice_in_dim(mask_one, panel_start, local_rows)[:, None]
    local_two = panel_two * lax.dynamic_slice_in_dim(mask_two, panel_start, local_rows)[:, None]
    result_mask_one = lax.dynamic_slice_in_dim(mask_one, result_start, local_rows)[:, None]
    result_mask_two = lax.dynamic_slice_in_dim(mask_two, result_start, local_rows)[:, None]

    both = jnp.concatenate([local_one, local_two], axis=1)
    moves = [(f, (f % row_count) * col_count + f // row_count) for f in range(row_count * col_count)]
    resident = lax.ppermute(both, ("row", "col"), moves)
    if local_rows % 128 == 0:
        high, low = gather_columns(both.T, col_count)
        product = product_rows(ancestor_inverse, high, low, row_count).T
    else:
        gathered = lax.all_gather(both, "col", axis=0, tiled=True)
        product = scatter_rows(contract_rows(ancestor_inverse, gathered, lax.Precision.HIGH), row_count)
    resident_one = resident[:, :width]
    resident_two = resident[:, width:]
    inverse_one = -product[:, :width] * result_mask_one
    inverse_two = -(product[:, width:] + matmul(inverse_one, panel_above)) * result_mask_two
    grams = (
        contract_rows(resident_one, inverse_one),
        contract_rows(inverse_one, resident_two),
        contract_rows(resident_two, inverse_two),
    )
    lanes = 128
    packed = jnp.concatenate(
        [gram[:, at : at + lanes] for gram in grams for at in range(0, width, lanes)], axis=0
    )
    sums = sum_everywhere(packed, row_count, col_count).reshape(len(grams), width // lanes, width, lanes)
    gram_one, cross_sum, gram_two = (
        jnp.concatenate([sums[at, block] for block in range(width // lanes)], axis=1) for at in range(len(grams))
    )
    diag_one = matmul(lower_one.T, lower_one) - gram_one
    cross_two = -(cross_sum + matmul(diag_one, panel_above))
    diag_two = matmul(lower_two.T, lower_two) - gram_two - matmul(panel_above.T, cross_two)
    delivered = deliver(inverse_two, tile_owner, col_count)
    return (inverse_one, diag_one, cross_two, diag_two, delivered)


def solution(mesh):
    return jax.shard_map(
        local,
        mesh=mesh,
        in_specs=(
            P("row", "col"),
            P(("row", "col"), None),
            P(),
            P(),
            P(("row", "col"), None),
            P(),
            P(),
            P(),
            P(("col", "row"), None),
        ),
        out_specs=(P(("col", "row"), None), P(), P(), P(), P(("row", "col"), None, None)),
        check_vma=False,
    )
```

```python
import functools

import jax
import jax.numpy as jnp
from jax import lax
from jax.experimental import pallas as pl
from jax.experimental.pallas import tpu as pltpu
from jax.sharding import PartitionSpec as P

CAP = 2


def matmul(left, right):
    return jnp.dot(left, right, precision=lax.Precision.HIGHEST, preferred_element_type=jnp.float32)


def contract_rows(left, right, precision=lax.Precision.HIGHEST):
    return lax.dot_general(
        left,
        right,
        (((0,), (0,)), ((), ())),
        precision=precision,
        preferred_element_type=jnp.float32,
    )


def row_mask(struct, count):
    lanes = 128
    high = struct // lanes
    low = struct % lanes
    high_hot = (jnp.arange(count // lanes, dtype=jnp.int32)[:, None] == high[None, :]).astype(jnp.bfloat16)
    low_hot = (jnp.arange(lanes, dtype=jnp.int32)[:, None] == low[None, :]).astype(jnp.bfloat16)
    counts = lax.dot_general(high_hot, low_hot, (((1,), (1,)), ((), ())), preferred_element_type=jnp.float32)
    return (counts > 0.5).astype(jnp.float32).reshape(count)


MESH = pl.DeviceIdType.MESH


def greet(peers):
    barrier = pltpu.get_barrier_semaphore()
    for peer in peers:
        pl.semaphore_signal(barrier, inc=1, device_id=peer, device_id_type=MESH)
    pl.semaphore_wait(barrier, len(peers))


def scatter_kernel(rows, value_ref, out_ref, pair_in, total, major_in, pair_send, pair_recv, major_send, major_recv):
    majors = rows // 2
    row = lax.axis_index("row")
    col = lax.axis_index("col")
    major, minor = row // 2, row % 2
    partner = (major * 2 + 1 - minor, col)

    def peer(offset):
        return (lax.rem(major + offset, majors) * 2 + minor, col)

    greet([partner] + [peer(offset) for offset in range(1, majors)])
    order = sorted(range(1, majors), key=lambda offset: -min(offset, majors - offset)) + [0]
    started = []
    pair_copies = {}
    for offset in order:
        target = lax.rem(major + offset, majors)
        copy = pltpu.make_async_remote_copy(
            src_ref=value_ref.at[target * 2 + 1 - minor],
            dst_ref=pair_in.at[offset],
            send_sem=pair_send.at[offset],
            recv_sem=pair_recv.at[offset],
            device_id=partner,
            device_id_type=MESH,
        )
        copy.start()
        pair_copies[offset] = copy
    for offset in order:
        target = lax.rem(major + offset, majors)
        pair_copies[offset].wait_recv()
        total[offset] = pair_in[offset] + value_ref[target * 2 + minor]
        if offset:
            copy = pltpu.make_async_remote_copy(
                src_ref=total.at[offset],
                dst_ref=major_in.at[offset - 1],
                send_sem=major_send.at[offset - 1],
                recv_sem=major_recv.at[offset - 1],
                device_id=peer(offset),
                device_id_type=MESH,
            )
            copy.start()
            started.append(copy)
    for copy in started:
        copy.wait_recv()
    result = total[0]
    for slot in range(majors - 1):
        result = result + major_in[slot]
    out_ref[...] = result
    for copy in started:
        copy.wait_send()
    for offset in order:
        pair_copies[offset].wait_send()


def scatter_rows(value, rows):
    chunk, width = value.shape[0] // rows, value.shape[1]
    majors = rows // 2
    dma = pltpu.SemaphoreType.DMA
    return pl.pallas_call(
        functools.partial(scatter_kernel, rows),
        out_shape=jax.ShapeDtypeStruct((chunk, width), jnp.float32),
        in_specs=[pl.BlockSpec(memory_space=pltpu.VMEM)],
        out_specs=pl.BlockSpec(memory_space=pltpu.VMEM),
        scratch_shapes=[
            pltpu.VMEM((majors, chunk, width), jnp.float32),
            pltpu.VMEM((majors, chunk, width), jnp.float32),
            pltpu.VMEM((majors - 1, chunk, width), jnp.float32),
            dma((majors,)),
            dma((majors,)),
            dma((majors - 1,)),
            dma((majors - 1,)),
        ],
        compiler_params=pltpu.CompilerParams(
            collective_id=0, has_side_effects=True, vmem_limit_bytes=40 * 2**20
        ),
    )(value.reshape(rows, chunk, width))


def gather_kernel(cols, parts, block_ref, high_ref, low_ref, held, pair_send, pair_recv, far_send, far_recv, relay_send, relay_recv):
    row = lax.axis_index("row")
    col = lax.axis_index("col")
    outer = cols // 2
    far, core = col // 2, col % 2
    partner = (row, far * 2 + 1 - core)

    def far_peer(offset):
        return (row, lax.rem(far + offset, outer) * 2 + core)

    greet([partner] + [far_peer(offset) for offset in range(1, outer)])

    def send(source, slot, part, target, send_sem, recv_sem):
        copy = pltpu.make_async_remote_copy(
            src_ref=source,
            dst_ref=held.at[slot, part],
            send_sem=send_sem,
            recv_sem=recv_sem,
            device_id=target,
            device_id_type=MESH,
        )
        copy.start()
        return copy

    far_copies = [
        (offset, part, send(
            block_ref.at[part], col, part, far_peer(offset), far_send.at[offset - 1, part], far_recv.at[offset - 1, part]
        ))
        for part in range(parts)
        for offset in range(1, outer)
    ]
    pair_copies = [
        send(block_ref.at[part], col, part, partner, pair_send.at[part], pair_recv.at[part]) for part in range(parts)
    ]
    relays = []
    for offset, part, copy in far_copies:
        copy.wait_recv()
        source = lax.rem(far - offset + outer, outer) * 2 + core
        relays.append(
            send(
                held.at[source, part],
                source,
                part,
                partner,
                relay_send.at[offset - 1, part],
                relay_recv.at[offset - 1, part],
            )
        )
    held[col] = block_ref[...]
    for copy in pair_copies + relays:
        copy.wait_recv()
    height, length = block_ref.shape[1:]
    for slot in range(cols):
        for part in range(parts):
            value = held[slot, part]
            high = value.astype(jnp.bfloat16)
            place = (pl.ds(part * height, height), pl.ds(slot * length, length))
            high_ref[place] = high
            low_ref[place] = (value - high.astype(jnp.float32)).astype(jnp.bfloat16)
    for copy in pair_copies + relays + [entry[2] for entry in far_copies]:
        copy.wait_send()


def gather_columns(block, cols):
    parts = 2
    width, length = block.shape
    outer = cols // 2
    dma = pltpu.SemaphoreType.DMA
    return pl.pallas_call(
        functools.partial(gather_kernel, cols, parts),
        out_shape=[jax.ShapeDtypeStruct((width, cols * length), jnp.bfloat16)] * 2,
        in_specs=[pl.BlockSpec(memory_space=pltpu.VMEM)],
        out_specs=[pl.BlockSpec(memory_space=pltpu.VMEM)] * 2,
        scratch_shapes=[pltpu.VMEM((cols, parts, width // parts, length), jnp.float32)]
        + [dma((parts,))] * 2
        + [dma((outer - 1, parts))] * 4,
        compiler_params=pltpu.CompilerParams(
            collective_id=2, has_side_effects=True, vmem_limit_bytes=24 * 2**20
        ),
    )(block.reshape(parts, width // parts, length))


def product_kernel(
    rows, matrix_ref, high_ref, low_ref, out_ref, window, mine, other, pair_in, major_in,
    window_sem, pair_send, pair_recv, major_send, major_recv,
):
    majors = rows // 2
    row = lax.axis_index("row")
    col = lax.axis_index("col")
    major, minor = row // 2, row % 2
    partner = (major * 2 + 1 - minor, col)
    span = out_ref.shape[1]

    upper, lower = major // 2, major % 2
    near = ((upper * 2 + 1 - lower) * 2 + minor, col)
    away = (((1 - upper) * 2 + lower) * 2 + minor, col)

    def fetch(step, which):
        target_upper = lax.rem(upper + 1 + step // 2, 2)
        target_lower = lax.rem(lower + 1 + step, 2)
        target = (target_upper * 2 + target_lower) * 2 + lax.rem(1 - minor + which, 2)
        return pltpu.make_async_copy(
            matrix_ref.at[:, pl.ds(pl.multiple_of(target * span, 128), span)],
            window.at[which],
            window_sem.at[which],
        )

    def pair_copy(step):
        return pltpu.make_async_remote_copy(
            src_ref=other.at[step],
            dst_ref=pair_in.at[step],
            send_sem=pair_send.at[step],
            recv_sem=pair_recv.at[step],
            device_id=partner,
            device_id_type=MESH,
        )

    for which in range(2):
        fetch(0, which).start()
    greet([partner, near, away])

    def dot(left, right):
        return jnp.dot(left, right, preferred_element_type=jnp.float32)

    def body(step, carry):
        for which, result in enumerate((other, mine)):
            fetch(step, which).wait()
            value = window[which]
            high = value.astype(jnp.bfloat16)
            low = (value - high.astype(jnp.float32)).astype(jnp.bfloat16)
            result[step] = dot(high_ref[...], high) + (dot(high_ref[...], low) + dot(low_ref[...], high))

            @pl.when(step + 1 < majors)
            def _():
                fetch(step + 1, which).start()

            if which == 0:
                pair_copy(step).start()
        return carry

    lax.fori_loop(0, majors, body, 0)

    def forward(source, slot, target):
        copy = pltpu.make_async_remote_copy(
            src_ref=mine.at[source],
            dst_ref=major_in.at[slot],
            send_sem=major_send.at[slot],
            recv_sem=major_recv.at[slot],
            device_id=target,
            device_id_type=MESH,
        )
        copy.start()
        return copy

    pair_copy(0).wait_recv()
    mine[0] = mine[0] + pair_in[0]
    both_bits = forward(0, 0, near)
    pair_copy(1).wait_recv()
    mine[1] = mine[1] + pair_in[1]
    both_bits.wait_recv()
    mine[1] = mine[1] + major_in[0]
    high_bit = forward(1, 1, away)
    pair_copy(2).wait_recv()
    mine[2] = mine[2] + pair_in[2]
    low_bit = forward(2, 2, near)
    pair_copy(3).wait_recv()
    mine[3] = mine[3] + pair_in[3]
    high_bit.wait_recv()
    low_bit.wait_recv()
    out_ref[...] = mine[3] + major_in[1] + major_in[2]
    for copy in (both_bits, high_bit, low_bit):
        copy.wait_send()
    for step in range(majors):
        pair_copy(step).wait_send()


def product_rows(matrix, high, low, rows):
    width = high.shape[0]
    depth = matrix.shape[0]
    span = matrix.shape[1] // rows
    majors = rows // 2
    dma = pltpu.SemaphoreType.DMA
    vmem = lambda *shape: pltpu.VMEM(shape, jnp.float32)
    return pl.pallas_call(
        functools.partial(product_kernel, rows),
        out_shape=jax.ShapeDtypeStruct((width, span), jnp.float32),
        in_specs=[pl.BlockSpec(memory_space=pl.ANY)] + [pl.BlockSpec(memory_space=pltpu.VMEM)] * 2,
        out_specs=pl.BlockSpec(memory_space=pltpu.VMEM),
        scratch_shapes=[
            vmem(2, depth, span),
            vmem(majors, width, span),
            vmem(majors, width, span),
            vmem(majors, width, span),
            vmem(majors - 1, width, span),
            dma((2,)),
            dma((majors,)),
            dma((majors,)),
            dma((majors - 1,)),
            dma((majors - 1,)),
        ],
        compiler_params=pltpu.CompilerParams(
            collective_id=0, has_side_effects=True, vmem_limit_bytes=48 * 2**20
        ),
        cost_estimate=pl.CostEstimate(
            flops=6 * matrix.size * width, bytes_accessed=10 * matrix.size, transcendentals=0
        ),
    )(matrix, high, low)


def sum_kernel(rows, cols, value_ref, out_ref, full, sum_a, sum_b, in_a, in_b, in_c, *sems):
    row = lax.axis_index("row")
    col = lax.axis_index("col")
    outer = cols // 2
    far, core = col // 2, col % 2
    half = outer * rows
    base_a = core * half
    base_b = base_a + far * rows
    base_c = base_b + row

    def pair_peer(offset):
        return (row, far * 2 + 1 - core)

    def far_peer(offset):
        return (row, lax.rem(far + offset, outer) * 2 + core)

    def row_peer(offset):
        return (lax.rem(row + offset, rows), col)

    greet(
        [pair_peer(1)]
        + [far_peer(offset) for offset in range(1, outer)]
        + [row_peer(offset) for offset in range(1, rows)]
    )

    def exchange(count, peer, source, landing, stage):
        copies = []
        for offset in range(1, count):
            copy = pltpu.make_async_remote_copy(
                src_ref=source(offset),
                dst_ref=landing(offset),
                send_sem=sems[2 * stage].at[offset - 1],
                recv_sem=sems[2 * stage + 1].at[offset - 1],
                device_id=peer(offset),
                device_id_type=MESH,
            )
            copy.start()
            copies.append(copy)
        for copy in copies:
            copy.wait_recv()
        return copies

    pending = []
    pending += exchange(
        2, pair_peer, lambda k: value_ref.at[pl.ds((1 - core) * half, half)], lambda k: in_a.at[k - 1], 0
    )
    sum_a[...] = value_ref[pl.ds(base_a, half)] + in_a[0]
    pending += exchange(
        outer, far_peer, lambda k: sum_a.at[pl.ds(lax.rem(far + k, outer) * rows, rows)], lambda k: in_b.at[k - 1], 1
    )
    total = sum_a[pl.ds(far * rows, rows)]
    for slot in range(outer - 1):
        total = total + in_b[slot]
    sum_b[...] = total
    pending += exchange(
        rows, row_peer, lambda k: sum_b.at[lax.rem(row + k, rows)], lambda k: in_c.at[k - 1], 2
    )
    total = sum_b[row]
    for slot in range(rows - 1):
        total = total + in_c[slot]
    full[base_c] = total
    pending += exchange(rows, row_peer, lambda k: full.at[base_c], lambda k: full.at[base_c], 3)
    pending += exchange(
        outer, far_peer, lambda k: full.at[pl.ds(base_b, rows)], lambda k: full.at[pl.ds(base_b, rows)], 4
    )
    pending += exchange(
        2, pair_peer, lambda k: full.at[pl.ds(base_a, half)], lambda k: full.at[pl.ds(base_a, half)], 5
    )
    out_ref[...] = full[...]
    for copy in pending:
        copy.wait_send()


def sum_everywhere(value, rows, cols):
    devices = rows * cols
    lanes = value.shape[1]
    depth = value.shape[0] // devices
    outer = cols // 2
    dma = pltpu.SemaphoreType.DMA
    vmem = lambda *lead: pltpu.VMEM(lead + (depth, lanes), jnp.float32)
    total = pl.pallas_call(
        functools.partial(sum_kernel, rows, cols),
        out_shape=jax.ShapeDtypeStruct((devices, depth, lanes), jnp.float32),
        in_specs=[pl.BlockSpec(memory_space=pltpu.VMEM)],
        out_specs=pl.BlockSpec(memory_space=pltpu.VMEM),
        scratch_shapes=[
            vmem(devices),
            vmem(devices // 2),
            vmem(rows),
            vmem(1, devices // 2),
            vmem(outer - 1, rows),
            vmem(rows - 1),
        ]
        + [dma((count - 1,)) for count in (2, outer, rows, rows, outer, 2) for _ in range(2)],
        compiler_params=pltpu.CompilerParams(
            collective_id=1, has_side_effects=True, vmem_limit_bytes=24 * 2**20
        ),
        cost_estimate=pl.CostEstimate(flops=0, bytes_accessed=100 * value.size * 4, transcendentals=0),
    )(value.reshape(devices, depth, lanes))
    return total.reshape(value.shape)


def deliver(values, tile_owner, col_count):
    tile_count = tile_owner.shape[0]
    tile_rows = values.shape[0] // tile_count
    all_tiles = values.reshape(tile_count, tile_rows, values.shape[1])
    owner_col = tile_owner[:, 0]
    col_ids = jnp.arange(col_count, dtype=jnp.int32)
    onehot = (owner_col[:, None] == col_ids[None, :]).astype(jnp.int32)
    tile_rank = jnp.sum((jnp.cumsum(onehot, axis=0) - onehot) * onehot, axis=1)
    slot_index = jnp.arange(CAP, dtype=jnp.int32)
    select = (
        (owner_col[None, None, :] == col_ids[:, None, None])
        & (tile_rank[None, None, :] == slot_index[None, :, None])
    ).astype(jnp.float32)
    outgoing = jnp.einsum("cks,srb->ckrb", select, all_tiles, precision=lax.Precision.HIGHEST)
    incoming = lax.all_to_all(outgoing, "col", split_axis=0, concat_axis=0, tiled=True)
    return incoming.reshape(col_count * CAP, tile_rows, values.shape[1])


def local(
    ancestor_inverse,
    panel_one,
    struct_one,
    lower_one,
    panel_two,
    struct_two,
    panel_above,
    lower_two,
    tile_owner,
):
    row_count = lax.axis_size("row")
    col_count = lax.axis_size("col")
    row_index = lax.axis_index("row")
    col_index = lax.axis_index("col")
    local_rows = panel_one.shape[0]
    order = local_rows * row_count * col_count
    width = panel_one.shape[1]
    mask_one = row_mask(struct_one, order)
    mask_two = row_mask(struct_two, order)
    panel_start = (row_index * col_count + col_index) * local_rows
    result_start = (col_index * row_count + row_index) * local_rows
    local_one = panel_one * lax.dynamic_slice_in_dim(mask_one, panel_start, local_rows)[:, None]
    local_two = panel_two * lax.dynamic_slice_in_dim(mask_two, panel_start, local_rows)[:, None]
    result_mask_one = lax.dynamic_slice_in_dim(mask_one, result_start, local_rows)[:, None]
    result_mask_two = lax.dynamic_slice_in_dim(mask_two, result_start, local_rows)[:, None]

    both = jnp.concatenate([local_one, local_two], axis=1)
    late = both
    if local_rows % 128 == 0 and row_count // 2 == 4:
        high, low = gather_columns(both.T, col_count)
        high, late = lax.optimization_barrier((high, both))
        product = product_rows(ancestor_inverse, high, low, row_count).T
    else:
        gathered = lax.all_gather(both, "col", axis=0, tiled=True)
        product = scatter_rows(contract_rows(ancestor_inverse, gathered, lax.Precision.HIGH), row_count)
    moves = [(f, (f % row_count) * col_count + f // row_count) for f in range(row_count * col_count)]
    resident = lax.ppermute(late, ("row", "col"), moves)
    resident_one = resident[:, :width]
    resident_two = resident[:, width:]
    inverse_one = -product[:, :width] * result_mask_one
    inverse_two = -(product[:, width:] + matmul(inverse_one, panel_above)) * result_mask_two
    grams = (
        contract_rows(resident_one, inverse_one),
        contract_rows(inverse_one, resident_two),
        contract_rows(resident_two, inverse_two),
    )
    lanes = 128
    packed = jnp.concatenate(
        [gram[:, at : at + lanes] for gram in grams for at in range(0, width, lanes)], axis=0
    )
    sums = sum_everywhere(packed, row_count, col_count).reshape(len(grams), width // lanes, width, lanes)
    gram_one, cross_sum, gram_two = (
        jnp.concatenate([sums[at, block] for block in range(width // lanes)], axis=1) for at in range(len(grams))
    )
    diag_one = matmul(lower_one.T, lower_one) - gram_one
    cross_two = -(cross_sum + matmul(diag_one, panel_above))
    diag_two = matmul(lower_two.T, lower_two) - gram_two - matmul(panel_above.T, cross_two)
    delivered = deliver(inverse_two, tile_owner, col_count)
    return (inverse_one, diag_one, cross_two, diag_two, delivered)


def solution(mesh):
    return jax.shard_map(
        local,
        mesh=mesh,
        in_specs=(
            P("row", "col"),
            P(("row", "col"), None),
            P(),
            P(),
            P(("row", "col"), None),
            P(),
            P(),
            P(),
            P(("col", "row"), None),
        ),
        out_specs=(P(("col", "row"), None), P(), P(), P(), P(("row", "col"), None, None)),
        check_vma=False,
    )
```
